32 devices in a mesh: groups: 2 (over x), seq: 16 (over z, y, core).
Axes of the slice: x: 2, y: 2, z: 4, core: 2. Of those that a mesh axis runs over, the one named last changes fastest.
Arguments:
- tokens: bfloat16 [32768, 1024], P(('groups', 'seq')), parts along dimension 0, may hold values from -6 to 6
- cotangent: bfloat16 [32768, 1024], P(('groups', 'seq')), parts along dimension 0, may hold values from -6 to 6
- gate_weight: bfloat16 [1024, 1024], P('seq'), may hold values from -0.1875 to 0.1875
- left_blocks: bfloat16 [32, 512, 512], P('seq'), may hold values from -0.25 to 0.25
- right_blocks: bfloat16 [512, 32, 32], P('seq'), may hold values from -1 to 1
Outputs:
- output: bfloat16 [32768, 1024], P(('groups', 'seq')), parts along dimension 0
- input_grad: bfloat16 [32768, 1024], P(('groups', 'seq')), parts along dimension 0
- gate_grad: float32 [2048, 1024], P(('groups', 'seq')), parts along dimension 0
- left_grad: bfloat16 [64, 512, 512], P(('groups', 'seq')), parts along dimension 0
- right_grad: bfloat16 [1024, 32, 32], P(('groups', 'seq')), parts along dimension 0
The draws below stay inside these ranges and needn't reach their ends.
There are 2 independent parts, one for each index of `groups`. The reference program is written for one: setup_inputs(seed, part) draws one part's arguments, and reference() takes and returns one part's arrays. A program takes and returns all parts, laid end to end along the dimension named above; an argument that names none is the same for every part. Nothing has to cross between parts.
All inputs are finite; a program needn't handle non-finite values.
Results may differ from the reference program's by a relative error of at most 0.0095.
Values may be sent and summed in bfloat16 or wider, within the bound.
A program may use at most 128 MiB of HBM per device.

```python
import jax
import jax.numpy as jnp

WIDTH = 1024
INNER = 512
OUTER = 32
TOKENS = 16384


def spiked(array, rng, source, target, blocks, factor):
    def block_of(dim):
        return (jnp.arange(array.shape[dim]) // (array.shape[dim] // blocks)).reshape((-1,) + (1,) * (array.ndim - 1 - dim))

    first = jax.random.permutation(rng, blocks)[block_of(target)]
    far = (block_of(target) + blocks // 2) % blocks
    return jnp.where((block_of(source) == first) | (block_of(source) == far), factor * array, array)


def block_scale(key, shape, cuts, least, high):
    loudness = 1.0
    for position, parts in cuts:
        steps = jax.random.uniform(jax.random.fold_in(jax.random.fold_in(key, 6), position), (parts,), jnp.float32, least / len(cuts), high / len(cuts))
        loudness = loudness * jnp.repeat(jnp.exp(steps), shape[position] // parts).reshape((-1,) + (1,) * (len(shape) - 1 - position))
    return loudness


def normal_values(own_key, shape, deviation, reach, split=(), kind=jnp.bfloat16):
    entries = deviation * jax.random.normal(own_key, shape, jnp.float32)
    if split:
        entries = entries * block_scale(own_key, shape, split, -0.22, 0.18)
    return jnp.clip(entries, -reach, reach).astype(kind)


def gaussian_with(stream_key, extent, scale, reach, pieces, heavy, held_as=jnp.bfloat16):
    drawn = scale * jax.random.normal(stream_key, extent, jnp.float32)
    if pieces:
        drawn = drawn * block_scale(stream_key, extent, pieces, -0.22, 0.18)
    return jnp.clip(spiked(drawn, jax.random.fold_in(stream_key, 3), *heavy), -reach, reach).astype(held_as)


def setup_inputs(seed: int = 0, part: int = 0) -> dict:
    key_of = jax.random.split(jax.random.key(seed), 6)
    part_keys = jax.random.split(jax.random.fold_in(key_of[5], part), 6)
    tokens = gaussian_with(part_keys[0], (TOKENS, WIDTH), 1.0, 6.0, ((0, 16),), (0, 1, 16, 2.0))
    cotangent = normal_values(part_keys[1], (TOKENS, WIDTH), 1.0, 6.0, ((0, 16),))
    gate_weight = normal_values(key_of[2], (WIDTH, WIDTH), WIDTH ** -0.5, 0.1875, ((0, 16),))
    left_blocks = normal_values(key_of[3], (OUTER, INNER, INNER), INNER ** -0.5, 0.25, ((0, 16),))
    right_blocks = normal_values(key_of[4], (INNER, OUTER, OUTER), OUTER ** -0.5, 1.0, ((0, 16),))
    return {"tokens": tokens, "cotangent": cotangent, "gate_weight": gate_weight, "left_blocks": left_blocks, "right_blocks": right_blocks}


def silu_slope(value):
    sig = jax.nn.sigmoid(value)
    return sig * (1.0 + value * (1.0 - sig))


def reference(tokens, cotangent, gate_weight, left_blocks, right_blocks):
    grid = tokens.reshape(OUTER, INNER, WIDTH).astype(jnp.float32)
    left_f = left_blocks.astype(jnp.float32)
    right_f = right_blocks.astype(jnp.float32)
    first = jnp.einsum('ajb,abc->ajc', left_f, grid).astype(jnp.bfloat16)
    second = jnp.einsum('bia,abc->ibc', right_f, first.astype(jnp.float32)).astype(jnp.bfloat16)
    gate = jnp.dot(tokens, gate_weight, preferred_element_type=jnp.float32).astype(jnp.bfloat16)
    gate_f = gate.reshape(OUTER, INNER, WIDTH).astype(jnp.float32)
    factor = jax.nn.silu(gate_f)
    second_f = second.astype(jnp.float32)
    output = (second_f * factor).astype(jnp.bfloat16)
    upstream = cotangent.reshape(OUTER, INNER, WIDTH).astype(jnp.float32)
    second_grad = (upstream * factor).astype(jnp.bfloat16)
    gate_delta = (upstream * second_f * silu_slope(gate_f)).astype(jnp.bfloat16)
    second_grad_f = second_grad.astype(jnp.float32)
    first_grad = jnp.einsum('bia,ibc->abc', right_f, second_grad_f).astype(jnp.bfloat16)
    scale_w = WIDTH ** -0.5
    right_grad = (jnp.einsum('ibc,abc->bia', second_grad_f, first.astype(jnp.float32)) * scale_w).astype(jnp.bfloat16)
    first_grad_f = first_grad.astype(jnp.float32)
    left_grad = (jnp.einsum('ajc,abc->ajb', first_grad_f, grid) * scale_w).astype(jnp.bfloat16)
    mixer_part = jnp.einsum('ajb,ajc->abc', left_f, first_grad_f).reshape(TOKENS, WIDTH)
    delta_flat = gate_delta.reshape(TOKENS, WIDTH)
    gate_part = jnp.dot(delta_flat, gate_weight.T, preferred_element_type=jnp.float32)
    input_grad = (mixer_part + gate_part).astype(jnp.bfloat16)
    gate_grad = jnp.dot(tokens.T, delta_flat, preferred_element_type=jnp.float32) * (TOKENS ** -0.5)
    return (output.reshape(TOKENS, WIDTH), input_grad, gate_grad, left_grad, right_grad)
```

```python
import functools

import jax
import jax.numpy as jnp
from jax import lax
from jax.experimental import pallas as pl
from jax.experimental.pallas import tpu as pltpu
from jax.sharding import PartitionSpec as P


def silu_slope(value):
    sig = jax.nn.sigmoid(value)
    return sig * (1.0 + value * (1.0 - sig))


def to_columns(values):
    return lax.all_to_all(values, "seq", split_axis=1, concat_axis=0, tiled=True)


def to_rows(values):
    return lax.all_to_all(values, "seq", split_axis=0, concat_axis=1, tiled=True)


def body(tokens, cotangent, gate_weight, left_blocks, right_blocks):
    seq_count = lax.axis_size("seq")
    local_blocks = left_blocks.shape[0]
    block_size = left_blocks.shape[1]
    tok_rows = tokens.shape[0]
    channels = tokens.shape[1]
    token_grid = tokens.reshape(local_blocks, block_size, channels)
    upstream = cotangent.reshape(local_blocks, block_size, channels)
    first = jnp.einsum(
        "ajb,abc->ajc", left_blocks, token_grid, preferred_element_type=jnp.float32
    ).astype(jnp.bfloat16)
    full_weight = lax.all_gather(gate_weight, "seq", axis=0, tiled=True)
    gate_sum = jnp.dot(tokens, full_weight, preferred_element_type=jnp.float32)
    gate = gate_sum.astype(jnp.bfloat16).reshape(local_blocks, block_size, channels)
    first_cols = to_columns(first)
    second_cols = jnp.einsum(
        "bia,abc->ibc", right_blocks, first_cols, preferred_element_type=jnp.float32
    ).astype(jnp.bfloat16)
    second = to_rows(second_cols)
    gate_f = gate.astype(jnp.float32)
    factor = jax.nn.silu(gate_f)
    second_f = second.astype(jnp.float32)
    upstream_f = upstream.astype(jnp.float32)
    output = (second_f * factor).astype(jnp.bfloat16)
    second_grad = (upstream_f * factor).astype(jnp.bfloat16)
    gate_delta = (upstream_f * second_f * silu_slope(gate_f)).astype(jnp.bfloat16)
    grad_cols = to_columns(second_grad)
    first_grad_cols = jnp.einsum(
        "bia,ibc->abc", right_blocks, grad_cols, preferred_element_type=jnp.float32
    ).astype(jnp.bfloat16)
    scale_w = channels ** (-0.5)
    right_grad = (
        jnp.einsum("ibc,abc->bia", grad_cols, first_cols, preferred_element_type=jnp.float32)
        * scale_w
    ).astype(jnp.bfloat16)
    first_grad = to_rows(first_grad_cols)
    left_grad = (
        jnp.einsum("ajc,abc->ajb", first_grad, token_grid, preferred_element_type=jnp.float32)
        * scale_w
    ).astype(jnp.bfloat16)
    mixer_part = jnp.einsum(
        "ajb,ajc->abc", left_blocks, first_grad, preferred_element_type=jnp.float32
    ).reshape(tok_rows, channels)
    delta_flat = gate_delta.reshape(tok_rows, channels)
    gate_part = jnp.einsum("tc,kc->tk", delta_flat, full_weight, preferred_element_type=jnp.float32)
    input_grad = (mixer_part + gate_part).astype(jnp.bfloat16)
    weight_term = jnp.einsum("tk,tc->kc", tokens, delta_flat, preferred_element_type=jnp.float32)
    gate_grad = lax.psum_scatter(weight_term, "seq", scatter_dimension=0, tiled=True)
    gate_grad = gate_grad * (tok_rows * seq_count) ** (-0.5)
    return (output.reshape(tok_rows, channels), input_grad, gate_grad, left_grad, right_grad)


F32 = jnp.float32
BF16 = jnp.bfloat16
ROWS = 16
PLANE = 4


def mixer_kernel(
    n, tok, cot, wsh, left, rk,
    out, igrad, ggrad, lgrad, rgrad,
    wf, first_s, sg_s, fc, gc, sc, fgc, sr, fr, gate, delta, part, wt, half, quarter, tail, mix,
    ssem, rsem, ws_sem, wr_sem, gs_sem, gr_sem,
):
    me = lax.axis_index("seq")
    zi, qi = me // PLANE, me % PLANE
    chunks = fc.shape[0]
    blocks, width = tok.shape[0], tok.shape[2]
    nz = n // PLANE
    deep = fc.shape[1] * ROWS
    tile = 256
    per = tile // ROWS
    row_tiles = tok.shape[1] // tile

    barrier = pltpu.get_barrier_semaphore()

    def greet(s, carry):
        pl.semaphore_signal(barrier, inc=1, device_id={"seq": (me + s) % n}, device_id_type=pl.DeviceIdType.MESH)
        return carry

    lax.fori_loop(1, n, greet, 0)
    pl.semaphore_wait(barrier, n - 1)

    def remote(src, dst, ss, rs, dev):
        return pltpu.make_async_remote_copy(
            src_ref=src, dst_ref=dst, send_sem=ss, recv_sem=rs,
            device_id={"seq": dev}, device_id_type=pl.DeviceIdType.MESH,
        )

    def to_cols(ph, k, src, dst, s):
        t = (s * 7) % n
        peer = (me + t) % n
        return remote(
            src.at[:, peer * chunks + k], dst.at[k, pl.ds(me * blocks, blocks)],
            ssem.at[ph, k, t], rsem.at[ph, k, t], peer,
        )

    def to_rows_(ph, k, src, dst, s):
        t = (s * 7) % n
        peer = (me + t) % n
        return remote(
            src.at[k, pl.ds(peer * blocks, blocks)], dst.at[:, me * chunks + k],
            ssem.at[ph, k, t], rsem.at[ph, k, t], peer,
        )

    def each(make, action):
        def step(s, carry):
            copy = make(s)
            if action == "start":
                copy.start()
            elif action == "recv":
                copy.wait_recv()
            else:
                copy.wait_send()
            return carry

        lax.fori_loop(1, n, step, 0)

    def w_z(d):
        return remote(wsh, wf.at[zi, qi], ws_sem.at[0, d], wr_sem.at[0, d], ((zi + d) % nz) * PLANE + qi)

    def w_q(d):
        return remote(wf.at[:, qi], wf.at[:, qi], ws_sem.at[1, d], wr_sem.at[1, d], zi * PLANE + (qi + d) % PLANE)

    for d in range(1, nz):
        w_z(d).start()
    wf[zi, qi] = wsh[...]

    def first_tile(t, carry):
        a, j = t // row_tiles, t % row_tiles
        prod = jnp.dot(left[a, pl.ds(j * tile, tile), :], tok[a], preferred_element_type=F32)
        first_s[a, pl.ds(j * per, per)] = prod.astype(BF16).reshape(per, ROWS, width)
        return carry

    lax.fori_loop(0, blocks * row_tiles, first_tile, 0)
    for d in range(1, nz):
        w_z(d).wait_recv()
    for d in range(1, PLANE):
        w_q(d).start()
    for k in range(chunks):
        each(functools.partial(to_cols, 0, k, first_s, fc), "start")
        fc[k, pl.ds(me * blocks, blocks)] = first_s[:, me * chunks + k]

    spread = (
        lax.broadcasted_iota(jnp.int32, (deep // ROWS, deep), 1) // ROWS
        == lax.broadcasted_iota(jnp.int32, (deep // ROWS, deep), 0)
    ).astype(F32).astype(BF16)
    same = (
        lax.broadcasted_iota(jnp.int32, (deep, deep), 0) % ROWS
        == lax.broadcasted_iota(jnp.int32, (deep, deep), 1) % ROWS
    )
    for k in range(chunks):
        wide = jnp.dot(rk[k], spread, preferred_element_type=F32)
        mix[k] = jnp.where(same, wide, 0.0).astype(BF16)

    for d in range(1, PLANE):
        w_q(d).wait_recv()

    def gate_tile(t, carry):
        a, j = t // row_tiles, t % row_tiles
        rows = pl.ds(j * tile, tile)
        weight = wf[...].reshape(width, width)
        g = jnp.dot(tok[a, rows, :], weight, preferred_element_type=F32).astype(BF16)
        gate[a, rows, :] = g
        gf = g.astype(F32)
        up = cot[a, rows, :].astype(F32) * (gf * jax.nn.sigmoid(gf))
        sg_s[a, pl.ds(j * per, per)] = up.astype(BF16).reshape(per, ROWS, width)
        return carry

    lax.fori_loop(0, blocks * row_tiles, gate_tile, 0)
    for k in range(chunks):
        each(functools.partial(to_cols, 1, k, sg_s, gc), "start")
        gc[k, pl.ds(me * blocks, blocks)] = sg_s[:, me * chunks + k]

    def mixed(k, src, dst, dims):
        def step(t, carry):
            cols = pl.ds(pl.multiple_of(t * tile, tile), tile)
            x = src[k, :, :, cols].reshape(deep, tile)
            y = lax.dot_general(mix[k], x, (dims, ((), ())), preferred_element_type=F32)
            dst[k, :, :, cols] = y.astype(BF16).reshape(deep // ROWS, ROWS, tile)
            return carry

        lax.fori_loop(0, width // tile, step, 0)

    for k in range(chunks):
        each(functools.partial(to_cols, 0, k, first_s, fc), "recv")
        mixed(k, fc, sc, ((1,), (0,)))
        each(functools.partial(to_rows_, 2, k, sc, sr), "start")
        sr[:, me * chunks + k] = sc[k, pl.ds(me * blocks, blocks)]
    for k in range(chunks):
        each(functools.partial(to_cols, 1, k, sg_s, gc), "recv")
        mixed(k, gc, fgc, ((0,), (0,)))
        each(functools.partial(to_rows_, 3, k, fgc, fr), "start")
        fr[:, me * chunks + k] = fgc[k, pl.ds(me * blocks, blocks)]

    scale_w = width ** (-0.5)
    for k in range(chunks):
        pairs = lax.dot_general(
            gc[k].reshape(deep, width), fc[k].reshape(deep, width),
            (((1,), (1,)), ((), ())), preferred_element_type=F32,
        )
        kept = jnp.where(same, pairs * scale_w, 0.0).astype(BF16)
        rgrad[k] = lax.dot_general(
            kept, spread, (((1,), (1,)), ((), ())), preferred_element_type=F32
        ).astype(BF16)

    for k in range(chunks):
        each(functools.partial(to_rows_, 2, k, sc, sr), "recv")

    def delta_tile(t, carry):
        a, j = t // row_tiles, t % row_tiles
        rows = pl.ds(j * tile, tile)
        gf = gate[a, rows, :].astype(F32)
        sig = jax.nn.sigmoid(gf)
        sec = sr[a, pl.ds(j * per, per)].reshape(tile, width).astype(F32)
        up = cot[a, rows, :].astype(F32)
        out[a, rows, :] = (sec * (gf * sig)).astype(BF16)
        delta[a, rows, :] = (up * sec * (sig * (1.0 + gf * (1.0 - sig)))).astype(BF16)
        return carry

    lax.fori_loop(0, blocks * row_tiles, delta_tile, 0)

    def weight_tile(z, carry):
        cols = pl.ds(pl.multiple_of(z * tile, tile), tile)
        tokens_2d = tok[:, :, cols].reshape(blocks * tok.shape[1], tile)
        delta_2d = delta[...].reshape(blocks * tok.shape[1], width)
        prod = lax.dot_general(tokens_2d, delta_2d, (((0,), (0,)), ((), ())), preferred_element_type=F32)
        wt[z] = prod.astype(BF16).reshape(PLANE, tile // PLANE, width)
        return carry

    lax.fori_loop(0, width // tile, weight_tile, 0)

    def g_q(d):
        peer = (qi + d) % PLANE
        return remote(wt.at[:, peer], half.at[d - 1], gs_sem.at[0, d], gr_sem.at[0, d], zi * PLANE + peer)

    def g_z(d):
        peer = (zi + d) % nz
        return remote(quarter.at[peer], tail.at[d - 1], gs_sem.at[1, d], gr_sem.at[1, d], peer * PLANE + qi)

    for d in range(1, PLANE):
        g_q(d).start()

    def part_tile(t, carry):
        a, j = t // row_tiles, t % row_tiles
        rows = pl.ds(j * tile, tile)
        weight = wf[...].reshape(width, width)
        part[a, rows, :] = lax.dot_general(
            delta[a, rows, :], weight, (((1,), (1,)), ((), ())), preferred_element_type=F32
        )
        return carry

    lax.fori_loop(0, blocks * row_tiles, part_tile, 0)

    for d in range(1, PLANE):
        g_q(d).wait_recv()

    def sum_tile(z, carry):
        total = wt[z, qi].astype(F32)
        for d in range(PLANE - 1):
            total = total + half[d, z].astype(F32)
        quarter[z] = total.astype(BF16)
        return carry

    lax.fori_loop(0, nz, sum_tile, 0)
    for d in range(1, nz):
        g_z(d).start()
    for d in range(1, nz):
        g_z(d).wait_recv()
    total = quarter[zi].astype(F32)
    for d in range(nz - 1):
        total = total + tail[d].astype(F32)
    ggrad[...] = total * (blocks * tok.shape[1] * n) ** (-0.5)

    for k in range(chunks):
        each(functools.partial(to_rows_, 3, k, fgc, fr), "recv")

    def last_tile(t, carry):
        a, j = t // row_tiles, t % row_tiles
        rows = pl.ds(pl.multiple_of(j * tile, tile), tile)
        lg = lax.dot_general(
            fr[a, pl.ds(j * per, per)].reshape(tile, width), tok[a],
            (((1,), (1,)), ((), ())), preferred_element_type=F32,
        )
        lgrad[a, rows, :] = (lg * scale_w).astype(BF16)
        mixer = lax.dot_general(
            left[a, :, rows], fr[a].reshape(tok.shape[1], width),
            (((0,), (0,)), ((), ())), preferred_element_type=F32,
        )
        igrad[a, rows, :] = (mixer + part[a, rows, :]).astype(BF16)
        return carry

    lax.fori_loop(0, blocks * row_tiles, last_tile, 0)

    for k in range(chunks):
        each(functools.partial(to_cols, 0, k, first_s, fc), "send")
        each(functools.partial(to_cols, 1, k, sg_s, gc), "send")
        each(functools.partial(to_rows_, 2, k, sc, sr), "send")
        each(functools.partial(to_rows_, 3, k, fgc, fr), "send")
    for d in range(1, nz):
        w_z(d).wait_send()
        g_z(d).wait_send()
    for d in range(1, PLANE):
        w_q(d).wait_send()
        g_q(d).wait_send()


def fused_body(n, tokens, cotangent, gate_weight, left_blocks, right_blocks):
    blocks, inner = left_blocks.shape[0], left_blocks.shape[1]
    own, outer = right_blocks.shape[0], right_blocks.shape[1]
    width = tokens.shape[1]
    chunks = own // ROWS
    groups = inner // ROWS
    deep = outer * ROWS
    nz = n // PLANE
    shard = width // n
    rk = right_blocks.reshape(chunks, ROWS, outer, outer).transpose(0, 2, 1, 3).reshape(chunks, deep, outer)
    rows = (blocks, inner, width)
    by_row = pltpu.VMEM((blocks, groups, ROWS, width), BF16)
    by_col = pltpu.VMEM((chunks, outer, ROWS, width), BF16)
    vmem = pl.BlockSpec(memory_space=pltpu.VMEM)
    out, igrad, ggrad, lgrad, rgrad = pl.pallas_call(
        functools.partial(mixer_kernel, n),
        out_shape=(
            jax.ShapeDtypeStruct(rows, BF16),
            jax.ShapeDtypeStruct(rows, BF16),
            jax.ShapeDtypeStruct((shard, width), F32),
            jax.ShapeDtypeStruct((blocks, inner, inner), BF16),
            jax.ShapeDtypeStruct((chunks, deep, outer), BF16),
        ),
        in_specs=[vmem] * 5,
        out_specs=[vmem] * 5,
        scratch_shapes=[
            pltpu.VMEM((nz, PLANE, shard, width), BF16),
            by_row, by_row, by_col, by_col, by_col, by_col, by_row, by_row,
            pltpu.VMEM(rows, BF16),
            pltpu.VMEM(rows, BF16),
            pltpu.VMEM(rows, F32),
            pltpu.VMEM((nz, PLANE, shard, width), BF16),
            pltpu.VMEM((PLANE - 1, nz, shard, width), BF16),
            pltpu.VMEM((nz, shard, width), BF16),
            pltpu.VMEM((nz - 1, shard, width), BF16),
            pltpu.VMEM((chunks, deep, deep), BF16),
            pltpu.SemaphoreType.DMA((4, chunks, n)),
            pltpu.SemaphoreType.DMA((4, chunks, n)),
            pltpu.SemaphoreType.DMA((2, PLANE)),
            pltpu.SemaphoreType.DMA((2, PLANE)),
            pltpu.SemaphoreType.DMA((2, PLANE)),
            pltpu.SemaphoreType.DMA((2, PLANE)),
        ],
        compiler_params=pltpu.CompilerParams(
            collective_id=0, has_side_effects=True, vmem_limit_bytes=60 * 2**20
        ),
    )(
        tokens.reshape(rows), cotangent.reshape(rows), gate_weight, left_blocks, rk
    )
    rgrad = rgrad.reshape(chunks, outer, ROWS, outer).transpose(0, 2, 1, 3).reshape(own, outer, outer)
    return (out.reshape(tokens.shape), igrad.reshape(tokens.shape), ggrad, lgrad, rgrad)


def chosen_body(tokens, cotangent, gate_weight, left_blocks, right_blocks):
    n = lax.axis_size("seq")
    own, width, inner = right_blocks.shape[0], tokens.shape[1], left_blocks.shape[1]
    if n == PLANE * PLANE and own % ROWS == 0 and width == 256 * PLANE and inner % 256 == 0:
        return fused_body(n, tokens, cotangent, gate_weight, left_blocks, right_blocks)
    return body(tokens, cotangent, gate_weight, left_blocks, right_blocks)


def solution(mesh):
    in_specs = (
        P(("groups", "seq"), None),
        P(("groups", "seq"), None),
        P("seq", None),
        P("seq", None, None),
        P("seq", None, None),
    )
    out_specs = (
        P(("groups", "seq"), None),
        P(("groups", "seq"), None),
        P(("groups", "seq"), None),
        P(("groups", "seq"), None, None),
        P(("groups", "seq"), None, None),
    )
    return jax.shard_map(chosen_body, mesh=mesh, in_specs=in_specs, out_specs=out_specs, check_vma=False)
```

```python
import functools

import jax
import jax.numpy as jnp
from jax import lax
from jax.experimental import pallas as pl
from jax.experimental.pallas import tpu as pltpu
from jax.sharding import PartitionSpec as P


def silu_slope(value):
    sig = jax.nn.sigmoid(value)
    return sig * (1.0 + value * (1.0 - sig))


def to_columns(values):
    return lax.all_to_all(values, "seq", split_axis=1, concat_axis=0, tiled=True)


def to_rows(values):
    return lax.all_to_all(values, "seq", split_axis=0, concat_axis=1, tiled=True)


def body(tokens, cotangent, gate_weight, left_blocks, right_blocks):
    seq_count = lax.axis_size("seq")
    local_blocks = left_blocks.shape[0]
    block_size = left_blocks.shape[1]
    tok_rows = tokens.shape[0]
    channels = tokens.shape[1]
    token_grid = tokens.reshape(local_blocks, block_size, channels)
    upstream = cotangent.reshape(local_blocks, block_size, channels)
    first = jnp.einsum(
        "ajb,abc->ajc", left_blocks, token_grid, preferred_element_type=jnp.float32
    ).astype(jnp.bfloat16)
    full_weight = lax.all_gather(gate_weight, "seq", axis=0, tiled=True)
    gate_sum = jnp.dot(tokens, full_weight, preferred_element_type=jnp.float32)
    gate = gate_sum.astype(jnp.bfloat16).reshape(local_blocks, block_size, channels)
    first_cols = to_columns(first)
    second_cols = jnp.einsum(
        "bia,abc->ibc", right_blocks, first_cols, preferred_element_type=jnp.float32
    ).astype(jnp.bfloat16)
    second = to_rows(second_cols)
    gate_f = gate.astype(jnp.float32)
    factor = jax.nn.silu(gate_f)
    second_f = second.astype(jnp.float32)
    upstream_f = upstream.astype(jnp.float32)
    output = (second_f * factor).astype(jnp.bfloat16)
    second_grad = (upstream_f * factor).astype(jnp.bfloat16)
    gate_delta = (upstream_f * second_f * silu_slope(gate_f)).astype(jnp.bfloat16)
    grad_cols = to_columns(second_grad)
    first_grad_cols = jnp.einsum(
        "bia,ibc->abc", right_blocks, grad_cols, preferred_element_type=jnp.float32
    ).astype(jnp.bfloat16)
    scale_w = channels ** (-0.5)
    right_grad = (
        jnp.einsum("ibc,abc->bia", grad_cols, first_cols, preferred_element_type=jnp.float32)
        * scale_w
    ).astype(jnp.bfloat16)
    first_grad = to_rows(first_grad_cols)
    left_grad = (
        jnp.einsum("ajc,abc->ajb", first_grad, token_grid, preferred_element_type=jnp.float32)
        * scale_w
    ).astype(jnp.bfloat16)
    mixer_part = jnp.einsum(
        "ajb,ajc->abc", left_blocks, first_grad, preferred_element_type=jnp.float32
    ).reshape(tok_rows, channels)
    delta_flat = gate_delta.reshape(tok_rows, channels)
    gate_part = jnp.einsum("tc,kc->tk", delta_flat, full_weight, preferred_element_type=jnp.float32)
    input_grad = (mixer_part + gate_part).astype(jnp.bfloat16)
    weight_term = jnp.einsum("tk,tc->kc", tokens, delta_flat, preferred_element_type=jnp.float32)
    gate_grad = lax.psum_scatter(weight_term, "seq", scatter_dimension=0, tiled=True)
    gate_grad = gate_grad * (tok_rows * seq_count) ** (-0.5)
    return (output.reshape(tok_rows, channels), input_grad, gate_grad, left_grad, right_grad)


F32 = jnp.float32
BF16 = jnp.bfloat16
ROWS = 16
PLANE = 4


def mixer_kernel(
    n, tok_hbm, cot_hbm, wsh, left_hbm, right,
    out_hbm, part_hbm, fr, ggrad, rgrad,
    tok, cot, left, out, part, wf, first_s, sg_s, fc, gc, sc, fgc, sr, gate, delta, wt, half, quarter, pair, tail, mix,
    ssem, rsem, ws_sem, wr_sem, gs_sem, gr_sem, lsem,
):
    me = lax.axis_index("seq")
    zi, qi = me // PLANE, me % PLANE
    chunks = fc.shape[0]
    blocks, width = tok.shape[0], tok.shape[2]
    nz = n // PLANE
    deep = fc.shape[1] * ROWS
    tile = 256
    per = tile // ROWS
    row_tiles = tok.shape[1] // tile

    loads = [
        pltpu.make_async_copy(left_hbm, left, lsem.at[0]),
        pltpu.make_async_copy(tok_hbm, tok, lsem.at[1]),
        pltpu.make_async_copy(wsh, wf.at[zi, qi], lsem.at[2]),
        pltpu.make_async_copy(cot_hbm, cot, lsem.at[3]),
    ]
    for load in loads:
        load.start()

    barrier = pltpu.get_barrier_semaphore()

    def greet(s, carry):
        pl.semaphore_signal(barrier, inc=1, device_id={"seq": (me + s) % n}, device_id_type=pl.DeviceIdType.MESH)
        return carry

    lax.fori_loop(1, n, greet, 0)
    pl.semaphore_wait(barrier, n - 1)

    def remote(src, dst, ss, rs, dev):
        return pltpu.make_async_remote_copy(
            src_ref=src, dst_ref=dst, send_sem=ss, recv_sem=rs,
            device_id={"seq": dev}, device_id_type=pl.DeviceIdType.MESH,
        )

    def to_cols(ph, k, src, dst, s):
        t = (s * 7) % n
        peer = (me + t) % n
        return remote(
            src.at[:, peer * chunks + k], dst.at[k, pl.ds(me * blocks, blocks)],
            ssem.at[ph, k, t], rsem.at[ph, k, t], peer,
        )

    def to_rows_(ph, k, src, dst, s):
        t = (s * 7) % n
        peer = (me + t) % n
        return remote(
            src.at[k, pl.ds(peer * blocks, blocks)], dst.at[:, me * chunks + k],
            ssem.at[ph, k, t], rsem.at[ph, k, t], peer,
        )

    def each(make, action):
        def step(s, carry):
            copy = make(s)
            if action == "start":
                copy.start()
            elif action == "recv":
                copy.wait_recv()
            else:
                copy.wait_send()
            return carry

        lax.fori_loop(1, n, step, 0)

    across = (zi + nz // 2) % nz
    beside = zi + 1 - 2 * (zi % 2)

    w_far = remote(wsh, wf.at[zi, qi], ws_sem.at[0, 0], wr_sem.at[0, 0], across * PLANE + qi)
    w_near = remote(wsh, wf.at[zi, qi], ws_sem.at[0, 1], wr_sem.at[0, 1], beside * PLANE + qi)
    w_pass = remote(wf.at[across, qi], wf.at[across, qi], ws_sem.at[0, 2], wr_sem.at[0, 2], beside * PLANE + qi)

    def w_q(d):
        return remote(wf.at[:, qi], wf.at[:, qi], ws_sem.at[1, d], wr_sem.at[1, d], zi * PLANE + (qi + d) % PLANE)

    w_far.start()
    w_near.start()
    loads[0].wait()
    loads[1].wait()

    def first_tile(t, carry):
        a, j = t // row_tiles, t % row_tiles
        prod = jnp.dot(left[a, pl.ds(j * tile, tile), :], tok[a], preferred_element_type=F32)
        first_s[a, pl.ds(j * per, per)] = prod.astype(BF16).reshape(per, ROWS, width)
        return carry

    lax.fori_loop(0, blocks * row_tiles, first_tile, 0)
    w_far.wait_recv()
    w_pass.start()
    for k in range(chunks):
        if k == 1:
            loads[2].wait()
            w_near.wait_recv()
            w_pass.wait_recv()
            for d in range(1, PLANE):
                w_q(d).start()
        each(functools.partial(to_cols, 0, k, first_s, fc), "start")
        fc[k, pl.ds(me * blocks, blocks)] = first_s[:, me * chunks + k]

    spread = (
        lax.broadcasted_iota(jnp.int32, (deep // ROWS, deep), 1) // ROWS
        == lax.broadcasted_iota(jnp.int32, (deep // ROWS, deep), 0)
    ).astype(F32).astype(BF16)
    same = (
        lax.broadcasted_iota(jnp.int32, (deep, deep), 0) % ROWS
        == lax.broadcasted_iota(jnp.int32, (deep, deep), 1) % ROWS
    )
    outer = deep // ROWS
    row = lax.broadcasted_iota(jnp.int32, (deep, deep), 0)
    col = lax.broadcasted_iota(jnp.int32, (deep, deep), 1)
    turn = ((row // ROWS == col % outer) & (row % ROWS == col // outer)).astype(F32).astype(BF16)
    for k in range(chunks):
        rk = jnp.dot(turn, right[k], preferred_element_type=F32).astype(BF16)
        wide = jnp.dot(rk, spread, preferred_element_type=F32)
        mix[k] = jnp.where(same, wide, 0.0).astype(BF16)

    for d in range(1, PLANE):
        w_q(d).wait_recv()
    loads[3].wait()

    def gate_tile(t, carry):
        a, j = t // row_tiles, t % row_tiles
        rows = pl.ds(j * tile, tile)
        weight = wf[...].reshape(width, width)
        g = jnp.dot(tok[a, rows, :], weight, preferred_element_type=F32).astype(BF16)
        gate[a, rows, :] = g
        gf = g.astype(F32)
        up = cot[a, rows, :].astype(F32) * (gf * jax.nn.sigmoid(gf))
        sg_s[a, pl.ds(j * per, per)] = up.astype(BF16).reshape(per, ROWS, width)
        return carry

    lax.fori_loop(0, blocks * row_tiles, gate_tile, 0)
    for k in range(chunks):
        each(functools.partial(to_cols, 1, k, sg_s, gc), "start")
        gc[k, pl.ds(me * blocks, blocks)] = sg_s[:, me * chunks + k]

    def mixed(k, src, dst, dims):
        def step(t, carry):
            cols = pl.ds(pl.multiple_of(t * tile, tile), tile)
            x = src[k, :, :, cols].reshape(deep, tile)
            y = lax.dot_general(mix[k], x, (dims, ((), ())), preferred_element_type=F32)
            dst[k, :, :, cols] = y.astype(BF16).reshape(deep // ROWS, ROWS, tile)
            return carry

        lax.fori_loop(0, width // tile, step, 0)

    for k in range(chunks):
        each(functools.partial(to_cols, 0, k, first_s, fc), "recv")
        mixed(k, fc, sc, ((1,), (0,)))
        each(functools.partial(to_rows_, 2, k, sc, sr), "start")
        sr[:, me * chunks + k] = sc[k, pl.ds(me * blocks, blocks)]
    for k in range(chunks):
        each(functools.partial(to_cols, 1, k, sg_s, gc), "recv")
        mixed(k, gc, fgc, ((0,), (0,)))
        each(functools.partial(to_rows_, 3, k, fgc, fr), "start")
        pltpu.make_async_copy(
            fgc.at[k, pl.ds(me * blocks, blocks)], fr.at[:, me * chunks + k], lsem.at[4 + k]
        ).start()

    scale_w = width ** (-0.5)
    for k in range(chunks):
        pairs = lax.dot_general(
            gc[k].reshape(deep, width), fc[k].reshape(deep, width),
            (((1,), (1,)), ((), ())), preferred_element_type=F32,
        )
        kept = jnp.where(same, pairs * scale_w, 0.0).astype(BF16)
        picked = lax.dot_general(
            kept, spread, (((1,), (1,)), ((), ())), preferred_element_type=F32
        ).astype(BF16)
        rgrad[k] = lax.dot_general(
            turn, picked, (((0,), (0,)), ((), ())), preferred_element_type=F32
        ).astype(BF16)

    for k in range(chunks):
        each(functools.partial(to_rows_, 2, k, sc, sr), "recv")

    def delta_tile(t, carry):
        a, j = t // row_tiles, t % row_tiles
        rows = pl.ds(j * tile, tile)
        gf = gate[a, rows, :].astype(F32)
        sig = jax.nn.sigmoid(gf)
        sec = sr[a, pl.ds(j * per, per)].reshape(tile, width).astype(F32)
        up = cot[a, rows, :].astype(F32)
        out[a, rows, :] = (sec * (gf * sig)).astype(BF16)
        delta[a, rows, :] = (up * sec * (sig * (1.0 + gf * (1.0 - sig)))).astype(BF16)
        return carry

    lax.fori_loop(0, blocks * row_tiles, delta_tile, 0)
    out_copy = pltpu.make_async_copy(out, out_hbm, lsem.at[0])
    out_copy.start()

    def weight_tile(z, carry):
        cols = pl.ds(pl.multiple_of(z * tile, tile), tile)
        tokens_2d = tok[:, :, cols].reshape(blocks * tok.shape[1], tile)
        delta_2d = delta[...].reshape(blocks * tok.shape[1], width)
        prod = lax.dot_general(tokens_2d, delta_2d, (((0,), (0,)), ((), ())), preferred_element_type=F32)
        wt[z] = prod.astype(BF16).reshape(PLANE, tile // PLANE, width)
        return carry

    lax.fori_loop(0, width // tile, weight_tile, 0)

    def g_q(d):
        peer = (qi + d) % PLANE
        return remote(wt.at[:, peer], half.at[d - 1], gs_sem.at[0, d], gr_sem.at[0, d], zi * PLANE + peer)

    g_near = [
        remote(quarter.at[beside], tail.at[0], gs_sem.at[1, 0], gr_sem.at[1, 0], beside * PLANE + qi),
        remote(
            quarter.at[(beside + nz // 2) % nz], tail.at[1], gs_sem.at[1, 1], gr_sem.at[1, 1], beside * PLANE + qi
        ),
    ]
    g_far = remote(pair, tail.at[2], gs_sem.at[1, 2], gr_sem.at[1, 2], across * PLANE + qi)

    for d in range(1, PLANE):
        g_q(d).start()

    def part_tile(t, carry):
        a, j = t // row_tiles, t % row_tiles
        rows = pl.ds(j * tile, tile)
        weight = wf[...].reshape(width, width)
        part[a, rows, :] = lax.dot_general(
            delta[a, rows, :], weight, (((1,), (1,)), ((), ())), preferred_element_type=F32
        ).astype(BF16)
        return carry

    lax.fori_loop(0, blocks * row_tiles, part_tile, 0)
    part_copy = pltpu.make_async_copy(part, part_hbm, lsem.at[1])
    part_copy.start()

    for d in range(1, PLANE):
        g_q(d).wait_recv()

    def sum_tile(z, carry):
        total = wt[z, qi].astype(F32)
        for d in range(PLANE - 1):
            total = total + half[d, z].astype(F32)
        quarter[z] = total.astype(BF16)
        return carry

    lax.fori_loop(0, nz, sum_tile, 0)
    for copy in g_near:
        copy.start()
    for copy in g_near:
        copy.wait_recv()
    pair[...] = (quarter[across].astype(F32) + tail[1].astype(F32)).astype(BF16)
    g_far.start()
    g_far.wait_recv()
    total = quarter[zi].astype(F32) + tail[0].astype(F32) + tail[2].astype(F32)
    ggrad[...] = total * (blocks * tok.shape[1] * n) ** (-0.5)

    for k in range(chunks):
        each(functools.partial(to_rows_, 3, k, fgc, fr), "recv")
        pltpu.make_async_copy(
            fgc.at[k, pl.ds(me * blocks, blocks)], fr.at[:, me * chunks + k], lsem.at[4 + k]
        ).wait()
    out_copy.wait()
    part_copy.wait()

    for k in range(chunks):
        each(functools.partial(to_cols, 0, k, first_s, fc), "send")
        each(functools.partial(to_cols, 1, k, sg_s, gc), "send")
        each(functools.partial(to_rows_, 2, k, sc, sr), "send")
        each(functools.partial(to_rows_, 3, k, fgc, fr), "send")
    for copy in (w_far, w_near, w_pass, *g_near, g_far):
        copy.wait_send()
    for d in range(1, PLANE):
        w_q(d).wait_send()
        g_q(d).wait_send()


def last_kernel(scale_w, tok, left, fr, part, out_in, ggrad_in, rgrad_in, out, igrad, lgrad, ggrad, rgrad):
    size = part.shape[1]
    rows = pl.ds(pl.multiple_of((pl.program_id(0) % (tok.shape[1] // size)) * size, size), size)
    out[...] = out_in[...]
    ggrad[...] = ggrad_in[...]
    rgrad[...] = rgrad_in[...]
    lg = lax.dot_general(fr[0, rows, :], tok[0], (((1,), (1,)), ((), ())), preferred_element_type=F32)
    lgrad[0] = (lg * scale_w).astype(BF16)
    mixer = lax.dot_general(left[0], fr[0], (((0,), (0,)), ((), ())), preferred_element_type=F32)
    igrad[0] = (mixer + part[0].astype(F32)).astype(BF16)


def fused_body(n, tokens, cotangent, gate_weight, left_blocks, right_blocks):
    blocks, inner = left_blocks.shape[0], left_blocks.shape[1]
    own, outer = right_blocks.shape[0], right_blocks.shape[1]
    width = tokens.shape[1]
    chunks = own // ROWS
    groups = inner // ROWS
    deep = outer * ROWS
    nz = n // PLANE
    shard = width // n
    rows = (blocks, inner, width)
    by_row = pltpu.VMEM((blocks, groups, ROWS, width), BF16)
    by_col = pltpu.VMEM((chunks, outer, ROWS, width), BF16)
    vmem = pl.BlockSpec(memory_space=pltpu.VMEM)
    hbm = pl.BlockSpec(memory_space=pltpu.HBM)
    token_grid = tokens.reshape(rows)
    out, part, fr, ggrad, rgrad = pl.pallas_call(
        functools.partial(mixer_kernel, n),
        out_shape=(
            jax.ShapeDtypeStruct(rows, BF16),
            jax.ShapeDtypeStruct(rows, BF16),
            jax.ShapeDtypeStruct((blocks, groups, ROWS, width), BF16),
            jax.ShapeDtypeStruct((shard, width), F32),
            jax.ShapeDtypeStruct((chunks, deep, outer), BF16),
        ),
        in_specs=[hbm, hbm, hbm, hbm, vmem],
        out_specs=[hbm, hbm, hbm, vmem, vmem],
        scratch_shapes=[
            pltpu.VMEM(rows, BF16),
            pltpu.VMEM(rows, BF16),
            pltpu.VMEM((blocks, inner, inner), BF16),
            pltpu.VMEM(rows, BF16),
            pltpu.VMEM(rows, BF16),
            pltpu.VMEM((nz, PLANE, shard, width), BF16),
            by_row, by_row, by_col, by_col, by_col, by_col, by_row,
            pltpu.VMEM(rows, BF16),
            pltpu.VMEM(rows, BF16),
            pltpu.VMEM((nz, PLANE, shard, width), BF16),
            pltpu.VMEM((PLANE - 1, nz, shard, width), BF16),
            pltpu.VMEM((nz, shard, width), BF16),
            pltpu.VMEM((shard, width), BF16),
            pltpu.VMEM((3, shard, width), BF16),
            pltpu.VMEM((chunks, deep, deep), BF16),
            pltpu.SemaphoreType.DMA((4, chunks, n)),
            pltpu.SemaphoreType.DMA((4, chunks, n)),
            pltpu.SemaphoreType.DMA((2, PLANE)),
            pltpu.SemaphoreType.DMA((2, PLANE)),
            pltpu.SemaphoreType.DMA((2, PLANE)),
            pltpu.SemaphoreType.DMA((2, PLANE)),
            pltpu.SemaphoreType.DMA((4 + chunks,)),
        ],
        compiler_params=pltpu.CompilerParams(
            collective_id=0, has_side_effects=True, vmem_limit_bytes=60 * 2**20
        ),
    )(
        token_grid, cotangent.reshape(rows), gate_weight, left_blocks, right_blocks.reshape(chunks, deep, outer)
    )
    size = 256
    per_block = inner // size
    steps = blocks * per_block
    tall = pl.BlockSpec((1, inner, width), lambda t: (t // per_block, 0, 0))
    flat = pl.BlockSpec((1, size, width), lambda t: (t // per_block, t % per_block, 0))
    square = pl.BlockSpec((1, size, inner), lambda t: (t // per_block, t % per_block, 0))
    side = pl.BlockSpec((1, inner, size), lambda t: (t // per_block, 0, t % per_block))
    weight_spec = pl.BlockSpec((shard // steps, width), lambda t: (t, 0))
    right_spec = pl.BlockSpec((own * outer // steps, outer), lambda t: (t, 0))
    out, igrad, lgrad, ggrad, rgrad = pl.pallas_call(
        functools.partial(last_kernel, width ** (-0.5)),
        grid=(steps,),
        out_shape=(
            jax.ShapeDtypeStruct(rows, BF16),
            jax.ShapeDtypeStruct(rows, BF16),
            jax.ShapeDtypeStruct((blocks, inner, inner), BF16),
            jax.ShapeDtypeStruct((shard, width), F32),
            jax.ShapeDtypeStruct((own * outer, outer), BF16),
        ),
        in_specs=[tall, side, tall, flat, flat, weight_spec, right_spec],
        out_specs=[flat, flat, square, weight_spec, right_spec],
    )(token_grid, left_blocks, fr.reshape(rows), part, out, ggrad, rgrad.reshape(own * outer, outer))
    rgrad = rgrad.reshape(own, outer, outer)
    return (out.reshape(tokens.shape), igrad.reshape(tokens.shape), ggrad, lgrad, rgrad)


def chosen_body(tokens, cotangent, gate_weight, left_blocks, right_blocks):
    n = lax.axis_size("seq")
    own, width, inner = right_blocks.shape[0], tokens.shape[1], left_blocks.shape[1]
    if n == PLANE * PLANE and own % ROWS == 0 and width == 256 * PLANE and inner % 256 == 0:
        return fused_body(n, tokens, cotangent, gate_weight, left_blocks, right_blocks)
    return body(tokens, cotangent, gate_weight, left_blocks, right_blocks)


def solution(mesh):
    in_specs = (
        P(("groups", "seq"), None),
        P(("groups", "seq"), None),
        P("seq", None),
        P("seq", None, None),
        P("seq", None, None),
    )
    out_specs = (
        P(("groups", "seq"), None),
        P(("groups", "seq"), None),
        P(("groups", "seq"), None),
        P(("groups", "seq"), None, None),
        P(("groups", "seq"), None, None),
    )
    return jax.shard_map(chosen_body, mesh=mesh, in_specs=in_specs, out_specs=out_specs, check_vma=False)
```

```python
import functools

import jax
import jax.numpy as jnp
from jax import lax
from jax.experimental import pallas as pl
from jax.experimental.pallas import tpu as pltpu
from jax.sharding import PartitionSpec as P


def silu_slope(value):
    sig = jax.nn.sigmoid(value)
    return sig * (1.0 + value * (1.0 - sig))


def to_columns(values):
    return lax.all_to_all(values, "seq", split_axis=1, concat_axis=0, tiled=True)


def to_rows(values):
    return lax.all_to_all(values, "seq", split_axis=0, concat_axis=1, tiled=True)


def body(tokens, cotangent, gate_weight, left_blocks, right_blocks):
    seq_count = lax.axis_size("seq")
    local_blocks = left_blocks.shape[0]
    block_size = left_blocks.shape[1]
    tok_rows = tokens.shape[0]
    channels = tokens.shape[1]
    token_grid = tokens.reshape(local_blocks, block_size, channels)
    upstream = cotangent.reshape(local_blocks, block_size, channels)
    first = jnp.einsum(
        "ajb,abc->ajc", left_blocks, token_grid, preferred_element_type=jnp.float32
    ).astype(jnp.bfloat16)
    full_weight = lax.all_gather(gate_weight, "seq", axis=0, tiled=True)
    gate_sum = jnp.dot(tokens, full_weight, preferred_element_type=jnp.float32)
    gate = gate_sum.astype(jnp.bfloat16).reshape(local_blocks, block_size, channels)
    first_cols = to_columns(first)
    second_cols = jnp.einsum(
        "bia,abc->ibc", right_blocks, first_cols, preferred_element_type=jnp.float32
    ).astype(jnp.bfloat16)
    second = to_rows(second_cols)
    gate_f = gate.astype(jnp.float32)
    factor = jax.nn.silu(gate_f)
    second_f = second.astype(jnp.float32)
    upstream_f = upstream.astype(jnp.float32)
    output = (second_f * factor).astype(jnp.bfloat16)
    second_grad = (upstream_f * factor).astype(jnp.bfloat16)
    gate_delta = (upstream_f * second_f * silu_slope(gate_f)).astype(jnp.bfloat16)
    grad_cols = to_columns(second_grad)
    first_grad_cols = jnp.einsum(
        "bia,ibc->abc", right_blocks, grad_cols, preferred_element_type=jnp.float32
    ).astype(jnp.bfloat16)
    scale_w = channels ** (-0.5)
    right_grad = (
        jnp.einsum("ibc,abc->bia", grad_cols, first_cols, preferred_element_type=jnp.float32)
        * scale_w
    ).astype(jnp.bfloat16)
    first_grad = to_rows(first_grad_cols)
    left_grad = (
        jnp.einsum("ajc,abc->ajb", first_grad, token_grid, preferred_element_type=jnp.float32)
        * scale_w
    ).astype(jnp.bfloat16)
    mixer_part = jnp.einsum(
        "ajb,ajc->abc", left_blocks, first_grad, preferred_element_type=jnp.float32
    ).reshape(tok_rows, channels)
    delta_flat = gate_delta.reshape(tok_rows, channels)
    gate_part = jnp.einsum("tc,kc->tk", delta_flat, full_weight, preferred_element_type=jnp.float32)
    input_grad = (mixer_part + gate_part).astype(jnp.bfloat16)
    weight_term = jnp.einsum("tk,tc->kc", tokens, delta_flat, preferred_element_type=jnp.float32)
    gate_grad = lax.psum_scatter(weight_term, "seq", scatter_dimension=0, tiled=True)
    gate_grad = gate_grad * (tok_rows * seq_count) ** (-0.5)
    return (output.reshape(tok_rows, channels), input_grad, gate_grad, left_grad, right_grad)


F32 = jnp.float32
BF16 = jnp.bfloat16
ROWS = 16
PLANE = 4


def mixer_kernel(
    n, tok_hbm, cot_hbm, wsh, left_hbm, right,
    out_hbm, part_hbm, fr, ggrad, rgrad,
    tok, cot, left, out, part, wf, first_s, sg_s, fc, gc, sc, fgc, sr, gate, delta, wt, half, quarter, pair, tail, mix,
    ssem, rsem, ws_sem, wr_sem, gs_sem, gr_sem, lsem,
):
    me = lax.axis_index("seq")
    zi, qi = me // PLANE, me % PLANE
    chunks = fc.shape[0]
    blocks, width = tok.shape[0], tok.shape[2]
    nz = n // PLANE
    deep = fc.shape[1] * ROWS
    tile = 256
    per = tile // ROWS
    row_tiles = tok.shape[1] // tile

    loads = [
        pltpu.make_async_copy(left_hbm, left, lsem.at[0]),
        pltpu.make_async_copy(tok_hbm, tok, lsem.at[1]),
        pltpu.make_async_copy(wsh, wf.at[zi, qi], lsem.at[2]),
        pltpu.make_async_copy(cot_hbm, cot, lsem.at[3]),
    ]
    for load in loads:
        load.start()

    barrier = pltpu.get_barrier_semaphore()

    def greet(s, carry):
        pl.semaphore_signal(barrier, inc=1, device_id={"seq": (me + s) % n}, device_id_type=pl.DeviceIdType.MESH)
        return carry

    lax.fori_loop(1, n, greet, 0)
    pl.semaphore_wait(barrier, n - 1)

    def remote(src, dst, ss, rs, dev):
        return pltpu.make_async_remote_copy(
            src_ref=src, dst_ref=dst, send_sem=ss, recv_sem=rs,
            device_id={"seq": dev}, device_id_type=pl.DeviceIdType.MESH,
        )

    def to_cols(ph, k, src, dst, s):
        t = (s * 7) % n
        peer = (me + t) % n
        return remote(
            src.at[:, peer * chunks + k], dst.at[k, pl.ds(me * blocks, blocks)],
            ssem.at[ph, k, t], rsem.at[ph, k, t], peer,
        )

    def to_rows_(ph, k, src, dst, s):
        t = (s * 7) % n
        peer = (me + t) % n
        return remote(
            src.at[k, pl.ds(peer * blocks, blocks)], dst.at[:, me * chunks + k],
            ssem.at[ph, k, t], rsem.at[ph, k, t], peer,
        )

    def each(make, action):
        def step(s, carry):
            copy = make(s)
            if action == "start":
                copy.start()
            elif action == "recv":
                copy.wait_recv()
            else:
                copy.wait_send()
            return carry

        lax.fori_loop(1, n, step, 0)

    across = (zi + nz // 2) % nz
    beside = zi + 1 - 2 * (zi % 2)

    w_far = remote(wsh, wf.at[zi, qi], ws_sem.at[0, 0], wr_sem.at[0, 0], across * PLANE + qi)
    w_near = remote(wsh, wf.at[zi, qi], ws_sem.at[0, 1], wr_sem.at[0, 1], beside * PLANE + qi)
    w_pass = remote(wf.at[across, qi], wf.at[across, qi], ws_sem.at[0, 2], wr_sem.at[0, 2], beside * PLANE + qi)

    def w_q(d):
        return remote(wf.at[:, qi], wf.at[:, qi], ws_sem.at[1, d], wr_sem.at[1, d], zi * PLANE + (qi + d) % PLANE)

    w_far.start()
    w_near.start()
    loads[0].wait()
    loads[1].wait()

    def first_tile(t, carry):
        a, j = t // row_tiles, t % row_tiles
        prod = jnp.dot(left[a, pl.ds(j * tile, tile), :], tok[a], preferred_element_type=F32)
        first_s[a, pl.ds(j * per, per)] = prod.astype(BF16).reshape(per, ROWS, width)
        return carry

    lax.fori_loop(0, blocks * row_tiles, first_tile, 0)
    def send_first(k):
        each(functools.partial(to_cols, 0, k, first_s, fc), "start")
        fc[k, pl.ds(me * blocks, blocks)] = first_s[:, me * chunks + k]

    def send_second_grad(k):
        each(functools.partial(to_cols, 1, k, sg_s, gc), "start")
        gc[k, pl.ds(me * blocks, blocks)] = sg_s[:, me * chunks + k]

    send_first(0)
    w_far.wait_recv()
    w_pass.start()
    for k in range(1, chunks):
        send_first(k)

    spread = (
        lax.broadcasted_iota(jnp.int32, (deep // ROWS, deep), 1) // ROWS
        == lax.broadcasted_iota(jnp.int32, (deep // ROWS, deep), 0)
    ).astype(F32).astype(BF16)
    same = (
        lax.broadcasted_iota(jnp.int32, (deep, deep), 0) % ROWS
        == lax.broadcasted_iota(jnp.int32, (deep, deep), 1) % ROWS
    )
    outer = deep // ROWS
    row = lax.broadcasted_iota(jnp.int32, (deep, deep), 0)
    col = lax.broadcasted_iota(jnp.int32, (deep, deep), 1)
    turn = ((row // ROWS == col % outer) & (row % ROWS == col // outer)).astype(F32).astype(BF16)
    for k in range(chunks):
        rk = jnp.dot(turn, right[k], preferred_element_type=F32).astype(BF16)
        wide = jnp.dot(rk, spread, preferred_element_type=F32)
        mix[k] = jnp.where(same, wide, 0.0).astype(BF16)

    def mixed(k, src, dst, dims):
        def step(t, carry):
            cols = pl.ds(pl.multiple_of(t * tile, tile), tile)
            x = src[k, :, :, cols].reshape(deep, tile)
            y = lax.dot_general(mix[k], x, (dims, ((), ())), preferred_element_type=F32)
            dst[k, :, :, cols] = y.astype(BF16).reshape(deep // ROWS, ROWS, tile)
            return carry

        lax.fori_loop(0, width // tile, step, 0)

    def second_of(k):
        each(functools.partial(to_cols, 0, k, first_s, fc), "recv")
        mixed(k, fc, sc, ((1,), (0,)))
        each(functools.partial(to_rows_, 2, k, sc, sr), "start")
        sr[:, me * chunks + k] = sc[k, pl.ds(me * blocks, blocks)]

    def first_grad_of(k):
        each(functools.partial(to_cols, 1, k, sg_s, gc), "recv")
        mixed(k, gc, fgc, ((0,), (0,)))
        each(functools.partial(to_rows_, 3, k, fgc, fr), "start")
        pltpu.make_async_copy(
            fgc.at[k, pl.ds(me * blocks, blocks)], fr.at[:, me * chunks + k], lsem.at[4 + k]
        ).start()

    second_of(0)
    loads[2].wait()
    w_near.wait_recv()
    w_pass.wait_recv()
    for d in range(1, PLANE):
        w_q(d).start()
    for k in range(1, chunks):
        second_of(k)

    for d in range(1, PLANE):
        w_q(d).wait_recv()
    loads[3].wait()

    def gate_tile(t, carry):
        a, j = t // row_tiles, t % row_tiles
        rows = pl.ds(j * tile, tile)
        weight = wf[...].reshape(width, width)
        g = jnp.dot(tok[a, rows, :], weight, preferred_element_type=F32).astype(BF16)
        gate[a, rows, :] = g
        gf = g.astype(F32)
        up = cot[a, rows, :].astype(F32) * (gf * jax.nn.sigmoid(gf))
        sg_s[a, pl.ds(j * per, per)] = up.astype(BF16).reshape(per, ROWS, width)
        return carry

    lax.fori_loop(0, blocks * row_tiles, gate_tile, 0)
    send_second_grad(0)

    for k in range(chunks):
        each(functools.partial(to_rows_, 2, k, sc, sr), "recv")

    def delta_tile(t, carry):
        a, j = t // row_tiles, t % row_tiles
        rows = pl.ds(j * tile, tile)
        gf = gate[a, rows, :].astype(F32)
        sig = jax.nn.sigmoid(gf)
        sec = sr[a, pl.ds(j * per, per)].reshape(tile, width).astype(F32)
        up = cot[a, rows, :].astype(F32)
        out[a, rows, :] = (sec * (gf * sig)).astype(BF16)
        delta[a, rows, :] = (up * sec * (sig * (1.0 + gf * (1.0 - sig)))).astype(BF16)
        return carry

    lax.fori_loop(0, blocks * row_tiles, delta_tile, 0)
    out_copy = pltpu.make_async_copy(out, out_hbm, lsem.at[0])
    out_copy.start()

    def weight_tile(z, carry):
        cols = pl.ds(pl.multiple_of(z * tile, tile), tile)
        tokens_2d = tok[:, :, cols].reshape(blocks * tok.shape[1], tile)
        delta_2d = delta[...].reshape(blocks * tok.shape[1], width)
        prod = lax.dot_general(tokens_2d, delta_2d, (((0,), (0,)), ((), ())), preferred_element_type=F32)
        wt[z] = prod.astype(BF16).reshape(PLANE, tile // PLANE, width)
        return carry

    lax.fori_loop(0, width // tile, weight_tile, 0)

    def g_q(d):
        peer = (qi + d) % PLANE
        return remote(wt.at[:, peer], half.at[d - 1], gs_sem.at[0, d], gr_sem.at[0, d], zi * PLANE + peer)

    g_near = [
        remote(quarter.at[beside], tail.at[0], gs_sem.at[1, 0], gr_sem.at[1, 0], beside * PLANE + qi),
        remote(
            quarter.at[(beside + nz // 2) % nz], tail.at[1], gs_sem.at[1, 1], gr_sem.at[1, 1], beside * PLANE + qi
        ),
    ]
    g_far = remote(pair, tail.at[2], gs_sem.at[1, 2], gr_sem.at[1, 2], across * PLANE + qi)

    for d in range(1, PLANE):
        g_q(d).start()

    for k in range(1, chunks):
        send_second_grad(k)

    for d in range(1, PLANE):
        g_q(d).wait_recv()

    def sum_tile(z, carry):
        total = wt[z, qi].astype(F32)
        for d in range(PLANE - 1):
            total = total + half[d, z].astype(F32)
        quarter[z] = total.astype(BF16)
        return carry

    lax.fori_loop(0, nz, sum_tile, 0)
    for copy in g_near:
        copy.start()
    first_grad_of(0)

    for copy in g_near:
        copy.wait_recv()
    pair[...] = (quarter[across].astype(F32) + tail[1].astype(F32)).astype(BF16)
    g_far.start()
    for k in range(1, chunks):
        first_grad_of(k)

    def part_tile(t, carry):
        a, j = t // row_tiles, t % row_tiles
        rows = pl.ds(j * tile, tile)
        weight = wf[...].reshape(width, width)
        part[a, rows, :] = lax.dot_general(
            delta[a, rows, :], weight, (((1,), (1,)), ((), ())), preferred_element_type=F32
        ).astype(BF16)
        return carry

    lax.fori_loop(0, blocks * row_tiles, part_tile, 0)
    part_copy = pltpu.make_async_copy(part, part_hbm, lsem.at[1])
    part_copy.start()

    scale_w = width ** (-0.5)
    for k in range(chunks):
        pairs = lax.dot_general(
            gc[k].reshape(deep, width), fc[k].reshape(deep, width),
            (((1,), (1,)), ((), ())), preferred_element_type=F32,
        )
        kept = jnp.where(same, pairs * scale_w, 0.0).astype(BF16)
        picked = lax.dot_general(
            kept, spread, (((1,), (1,)), ((), ())), preferred_element_type=F32
        ).astype(BF16)
        rgrad[k] = lax.dot_general(
            turn, picked, (((0,), (0,)), ((), ())), preferred_element_type=F32
        ).astype(BF16)

    g_far.wait_recv()
    total = quarter[zi].astype(F32) + tail[0].astype(F32) + tail[2].astype(F32)
    ggrad[...] = total * (blocks * tok.shape[1] * n) ** (-0.5)

    for k in range(chunks):
        each(functools.partial(to_rows_, 3, k, fgc, fr), "recv")
        pltpu.make_async_copy(
            fgc.at[k, pl.ds(me * blocks, blocks)], fr.at[:, me * chunks + k], lsem.at[4 + k]
        ).wait()
    out_copy.wait()
    part_copy.wait()

    for k in range(chunks):
        each(functools.partial(to_cols, 0, k, first_s, fc), "send")
        each(functools.partial(to_cols, 1, k, sg_s, gc), "send")
        each(functools.partial(to_rows_, 2, k, sc, sr), "send")
        each(functools.partial(to_rows_, 3, k, fgc, fr), "send")
    for copy in (w_far, w_near, w_pass, *g_near, g_far):
        copy.wait_send()
    for d in range(1, PLANE):
        w_q(d).wait_send()
        g_q(d).wait_send()


def last_kernel(scale_w, tok, left, fr, part, out_in, ggrad_in, rgrad_in, out, igrad, lgrad, ggrad, rgrad):
    size = part.shape[1]
    rows = pl.ds(pl.multiple_of((pl.program_id(0) % (tok.shape[1] // size)) * size, size), size)
    out[...] = out_in[...]
    ggrad[...] = ggrad_in[...]
    rgrad[...] = rgrad_in[...]
    lg = lax.dot_general(fr[0, rows, :], tok[0], (((1,), (1,)), ((), ())), preferred_element_type=F32)
    lgrad[0] = (lg * scale_w).astype(BF16)
    mixer = lax.dot_general(left[0], fr[0], (((0,), (0,)), ((), ())), preferred_element_type=F32)
    igrad[0] = (mixer + part[0].astype(F32)).astype(BF16)


def fused_body(n, tokens, cotangent, gate_weight, left_blocks, right_blocks):
    blocks, inner = left_blocks.shape[0], left_blocks.shape[1]
    own, outer = right_blocks.shape[0], right_blocks.shape[1]
    width = tokens.shape[1]
    chunks = own // ROWS
    groups = inner // ROWS
    deep = outer * ROWS
    nz = n // PLANE
    shard = width // n
    rows = (blocks, inner, width)
    by_row = pltpu.VMEM((blocks, groups, ROWS, width), BF16)
    by_col = pltpu.VMEM((chunks, outer, ROWS, width), BF16)
    vmem = pl.BlockSpec(memory_space=pltpu.VMEM)
    hbm = pl.BlockSpec(memory_space=pltpu.HBM)
    token_grid = tokens.reshape(rows)
    out, part, fr, ggrad, rgrad = pl.pallas_call(
        functools.partial(mixer_kernel, n),
        out_shape=(
            jax.ShapeDtypeStruct(rows, BF16),
            jax.ShapeDtypeStruct(rows, BF16),
            jax.ShapeDtypeStruct((blocks, groups, ROWS, width), BF16),
            jax.ShapeDtypeStruct((shard, width), F32),
            jax.ShapeDtypeStruct((chunks, deep, outer), BF16),
        ),
        in_specs=[hbm, hbm, hbm, hbm, vmem],
        out_specs=[hbm, hbm, hbm, vmem, vmem],
        scratch_shapes=[
            pltpu.VMEM(rows, BF16),
            pltpu.VMEM(rows, BF16),
            pltpu.VMEM((blocks, inner, inner), BF16),
            pltpu.VMEM(rows, BF16),
            pltpu.VMEM(rows, BF16),
            pltpu.VMEM((nz, PLANE, shard, width), BF16),
            by_row, by_row, by_col, by_col, by_col, by_col, by_row,
            pltpu.VMEM(rows, BF16),
            pltpu.VMEM(rows, BF16),
            pltpu.VMEM((nz, PLANE, shard, width), BF16),
            pltpu.VMEM((PLANE - 1, nz, shard, width), BF16),
            pltpu.VMEM((nz, shard, width), BF16),
            pltpu.VMEM((shard, width), BF16),
            pltpu.VMEM((3, shard, width), BF16),
            pltpu.VMEM((chunks, deep, deep), BF16),
            pltpu.SemaphoreType.DMA((4, chunks, n)),
            pltpu.SemaphoreType.DMA((4, chunks, n)),
            pltpu.SemaphoreType.DMA((2, PLANE)),
            pltpu.SemaphoreType.DMA((2, PLANE)),
            pltpu.SemaphoreType.DMA((2, PLANE)),
            pltpu.SemaphoreType.DMA((2, PLANE)),
            pltpu.SemaphoreType.DMA((4 + chunks,)),
        ],
        compiler_params=pltpu.CompilerParams(
            collective_id=0, has_side_effects=True, vmem_limit_bytes=60 * 2**20
        ),
    )(
        token_grid, cotangent.reshape(rows), gate_weight, left_blocks, right_blocks.reshape(chunks, deep, outer)
    )
    size = 256
    per_block = inner // size
    steps = blocks * per_block
    tall = pl.BlockSpec((1, inner, width), lambda t: (t // per_block, 0, 0))
    flat = pl.BlockSpec((1, size, width), lambda t: (t // per_block, t % per_block, 0))
    square = pl.BlockSpec((1, size, inner), lambda t: (t // per_block, t % per_block, 0))
    side = pl.BlockSpec((1, inner, size), lambda t: (t // per_block, 0, t % per_block))
    weight_spec = pl.BlockSpec((shard // steps, width), lambda t: (t, 0))
    right_spec = pl.BlockSpec((own * outer // steps, outer), lambda t: (t, 0))
    out, igrad, lgrad, ggrad, rgrad = pl.pallas_call(
        functools.partial(last_kernel, width ** (-0.5)),
        grid=(steps,),
        out_shape=(
            jax.ShapeDtypeStruct(rows, BF16),
            jax.ShapeDtypeStruct(rows, BF16),
            jax.ShapeDtypeStruct((blocks, inner, inner), BF16),
            jax.ShapeDtypeStruct((shard, width), F32),
            jax.ShapeDtypeStruct((own * outer, outer), BF16),
        ),
        in_specs=[tall, side, tall, flat, flat, weight_spec, right_spec],
        out_specs=[flat, flat, square, weight_spec, right_spec],
    )(token_grid, left_blocks, fr.reshape(rows), part, out, ggrad, rgrad.reshape(own * outer, outer))
    rgrad = rgrad.reshape(own, outer, outer)
    return (out.reshape(tokens.shape), igrad.reshape(tokens.shape), ggrad, lgrad, rgrad)


def chosen_body(tokens, cotangent, gate_weight, left_blocks, right_blocks):
    n = lax.axis_size("seq")
    own, width, inner = right_blocks.shape[0], tokens.shape[1], left_blocks.shape[1]
    if n == PLANE * PLANE and own % ROWS == 0 and width == 256 * PLANE and inner % 256 == 0:
        return fused_body(n, tokens, cotangent, gate_weight, left_blocks, right_blocks)
    return body(tokens, cotangent, gate_weight, left_blocks, right_blocks)


def solution(mesh):
    in_specs = (
        P(("groups", "seq"), None),
        P(("groups", "seq"), None),
        P("seq", None),
        P("seq", None, None),
        P("seq", None, None),
    )
    out_specs = (
        P(("groups", "seq"), None),
        P(("groups", "seq"), None),
        P(("groups", "seq"), None),
        P(("groups", "seq"), None, None),
        P(("groups", "seq"), None, None),
    )
    return jax.shard_map(chosen_body, mesh=mesh, in_specs=in_specs, out_specs=out_specs, check_vma=False)
```

```python
import functools

import jax
import jax.numpy as jnp
from jax import lax
from jax.experimental import pallas as pl
from jax.experimental.pallas import tpu as pltpu
from jax.sharding import PartitionSpec as P


def silu_slope(value):
    sig = jax.nn.sigmoid(value)
    return sig * (1.0 + value * (1.0 - sig))


def to_columns(values):
    return lax.all_to_all(values, "seq", split_axis=1, concat_axis=0, tiled=True)


def to_rows(values):
    return lax.all_to_all(values, "seq", split_axis=0, concat_axis=1, tiled=True)


def body(tokens, cotangent, gate_weight, left_blocks, right_blocks):
    seq_count = lax.axis_size("seq")
    local_blocks = left_blocks.shape[0]
    block_size = left_blocks.shape[1]
    tok_rows = tokens.shape[0]
    channels = tokens.shape[1]
    token_grid = tokens.reshape(local_blocks, block_size, channels)
    upstream = cotangent.reshape(local_blocks, block_size, channels)
    first = jnp.einsum(
        "ajb,abc->ajc", left_blocks, token_grid, preferred_element_type=jnp.float32
    ).astype(jnp.bfloat16)
    full_weight = lax.all_gather(gate_weight, "seq", axis=0, tiled=True)
    gate_sum = jnp.dot(tokens, full_weight, preferred_element_type=jnp.float32)
    gate = gate_sum.astype(jnp.bfloat16).reshape(local_blocks, block_size, channels)
    first_cols = to_columns(first)
    second_cols = jnp.einsum(
        "bia,abc->ibc", right_blocks, first_cols, preferred_element_type=jnp.float32
    ).astype(jnp.bfloat16)
    second = to_rows(second_cols)
    gate_f = gate.astype(jnp.float32)
    factor = jax.nn.silu(gate_f)
    second_f = second.astype(jnp.float32)
    upstream_f = upstream.astype(jnp.float32)
    output = (second_f * factor).astype(jnp.bfloat16)
    second_grad = (upstream_f * factor).astype(jnp.bfloat16)
    gate_delta = (upstream_f * second_f * silu_slope(gate_f)).astype(jnp.bfloat16)
    grad_cols = to_columns(second_grad)
    first_grad_cols = jnp.einsum(
        "bia,ibc->abc", right_blocks, grad_cols, preferred_element_type=jnp.float32
    ).astype(jnp.bfloat16)
    scale_w = channels ** (-0.5)
    right_grad = (
        jnp.einsum("ibc,abc->bia", grad_cols, first_cols, preferred_element_type=jnp.float32)
        * scale_w
    ).astype(jnp.bfloat16)
    first_grad = to_rows(first_grad_cols)
    left_grad = (
        jnp.einsum("ajc,abc->ajb", first_grad, token_grid, preferred_element_type=jnp.float32)
        * scale_w
    ).astype(jnp.bfloat16)
    mixer_part = jnp.einsum(
        "ajb,ajc->abc", left_blocks, first_grad, preferred_element_type=jnp.float32
    ).reshape(tok_rows, channels)
    delta_flat = gate_delta.reshape(tok_rows, channels)
    gate_part = jnp.einsum("tc,kc->tk", delta_flat, full_weight, preferred_element_type=jnp.float32)
    input_grad = (mixer_part + gate_part).astype(jnp.bfloat16)
    weight_term = jnp.einsum("tk,tc->kc", tokens, delta_flat, preferred_element_type=jnp.float32)
    gate_grad = lax.psum_scatter(weight_term, "seq", scatter_dimension=0, tiled=True)
    gate_grad = gate_grad * (tok_rows * seq_count) ** (-0.5)
    return (output.reshape(tok_rows, channels), input_grad, gate_grad, left_grad, right_grad)


F32 = jnp.float32
BF16 = jnp.bfloat16
ROWS = 16
PLANE = 4


def mixer_kernel(
    n, tok_hbm, cot_hbm, wsh, left_hbm, right,
    out_hbm, part_hbm, fr, ggrad, rgrad,
    tok, cot, left, out, part, wf, first_s, sg_s, fc, gc, sc, fgc, sr, gate, delta, wt, half, quarter, pair, tail, mix,
    ssem, rsem, ws_sem, wr_sem, gs_sem, gr_sem, lsem,
):
    me = lax.axis_index("seq")
    zi, qi = me // PLANE, me % PLANE
    chunks = fc.shape[0]
    blocks, width = tok.shape[0], tok.shape[2]
    nz = n // PLANE
    deep = fc.shape[1] * ROWS
    tile = 256
    per = tile // ROWS
    row_tiles = tok.shape[1] // tile

    loads = [
        pltpu.make_async_copy(left_hbm, left, lsem.at[0]),
        pltpu.make_async_copy(tok_hbm, tok, lsem.at[1]),
        pltpu.make_async_copy(wsh, wf.at[zi, qi], lsem.at[2]),
        pltpu.make_async_copy(cot_hbm, cot, lsem.at[3]),
    ]
    for load in loads:
        load.start()

    barrier = pltpu.get_barrier_semaphore()

    def greet(s, carry):
        pl.semaphore_signal(barrier, inc=1, device_id={"seq": (me + s) % n}, device_id_type=pl.DeviceIdType.MESH)
        return carry

    lax.fori_loop(1, n, greet, 0)
    pl.semaphore_wait(barrier, n - 1)

    def remote(src, dst, ss, rs, dev):
        return pltpu.make_async_remote_copy(
            src_ref=src, dst_ref=dst, send_sem=ss, recv_sem=rs,
            device_id={"seq": dev}, device_id_type=pl.DeviceIdType.MESH,
        )

    def to_cols(ph, k, src, dst, s):
        t = (s * 7) % n
        peer = (me + t) % n
        return remote(
            src.at[:, peer, k], dst.at[k, pl.ds(me * blocks, blocks)],
            ssem.at[ph, k, t], rsem.at[ph, k, t], peer,
        )

    def to_rows_(ph, k, src, dst, s):
        t = (s * 7) % n
        peer = (me + t) % n
        return remote(
            src.at[k, pl.ds(peer * blocks, blocks)], dst.at[:, me * chunks + k],
            ssem.at[ph, k, t], rsem.at[ph, k, t], peer,
        )

    def each(make, action):
        def step(s, carry):
            copy = make(s)
            if action == "start":
                copy.start()
            elif action == "recv":
                copy.wait_recv()
            else:
                copy.wait_send()
            return carry

        lax.fori_loop(1, n, step, 0)

    across = (zi + nz // 2) % nz
    beside = zi + 1 - 2 * (zi % 2)

    w_far = remote(wsh, wf.at[zi, qi], ws_sem.at[0, 0], wr_sem.at[0, 0], across * PLANE + qi)
    w_near = remote(wsh, wf.at[zi, qi], ws_sem.at[0, 1], wr_sem.at[0, 1], beside * PLANE + qi)
    w_pass = remote(wf.at[across, qi], wf.at[across, qi], ws_sem.at[0, 2], wr_sem.at[0, 2], beside * PLANE + qi)

    def w_q(d):
        return remote(wf.at[:, qi], wf.at[:, qi], ws_sem.at[1, d], wr_sem.at[1, d], zi * PLANE + (qi + d) % PLANE)

    w_far.start()
    w_near.start()
    loads[0].wait()
    loads[1].wait()

    def first_tile(k):
        def step(a, carry):
            lhs = left[a, :, k].reshape(n * ROWS, left.shape[4])
            prod = jnp.dot(lhs, tok[a], preferred_element_type=F32)
            first_s[a, :, k] = prod.astype(BF16).reshape(n, ROWS, width)
            return carry

        lax.fori_loop(0, blocks, step, 0)

    def send_first(k):
        first_tile(k)
        each(functools.partial(to_cols, 0, k, first_s, fc), "start")
        fc[k, pl.ds(me * blocks, blocks)] = first_s[:, me, k]

    def send_second_grad(k):
        each(functools.partial(to_cols, 1, k, sg_s, gc), "start")
        gc[k, pl.ds(me * blocks, blocks)] = sg_s[:, me, k]

    send_first(0)
    w_far.wait_recv()
    w_pass.start()
    for k in range(1, chunks):
        send_first(k)

    spread = (
        lax.broadcasted_iota(jnp.int32, (deep // ROWS, deep), 1) // ROWS
        == lax.broadcasted_iota(jnp.int32, (deep // ROWS, deep), 0)
    ).astype(F32).astype(BF16)
    same = (
        lax.broadcasted_iota(jnp.int32, (deep, deep), 0) % ROWS
        == lax.broadcasted_iota(jnp.int32, (deep, deep), 1) % ROWS
    )
    outer = deep // ROWS
    row = lax.broadcasted_iota(jnp.int32, (deep, deep), 0)
    col = lax.broadcasted_iota(jnp.int32, (deep, deep), 1)
    turn = ((row // ROWS == col % outer) & (row % ROWS == col // outer)).astype(F32).astype(BF16)
    for k in range(chunks):
        rk = jnp.dot(turn, right[k], preferred_element_type=F32).astype(BF16)
        wide = jnp.dot(rk, spread, preferred_element_type=F32)
        mix[k] = jnp.where(same, wide, 0.0).astype(BF16)

    def mixed(k, src, dst, dims):
        def step(t, carry):
            cols = pl.ds(pl.multiple_of(t * tile, tile), tile)
            x = src[k, :, :, cols].reshape(deep, tile)
            y = lax.dot_general(mix[k], x, (dims, ((), ())), preferred_element_type=F32)
            dst[k, :, :, cols] = y.astype(BF16).reshape(deep // ROWS, ROWS, tile)
            return carry

        lax.fori_loop(0, width // tile, step, 0)

    def second_of(k):
        each(functools.partial(to_cols, 0, k, first_s, fc), "recv")
        mixed(k, fc, sc, ((1,), (0,)))
        each(functools.partial(to_rows_, 2, k, sc, sr), "start")
        sr[:, me * chunks + k] = sc[k, pl.ds(me * blocks, blocks)]

    def first_grad_of(k):
        each(functools.partial(to_cols, 1, k, sg_s, gc), "recv")
        mixed(k, gc, fgc, ((0,), (0,)))
        each(functools.partial(to_rows_, 3, k, fgc, fr), "start")
        pltpu.make_async_copy(
            fgc.at[k, pl.ds(me * blocks, blocks)], fr.at[:, me * chunks + k], lsem.at[4 + k]
        ).start()

    second_of(0)
    loads[2].wait()
    w_near.wait_recv()
    w_pass.wait_recv()
    for d in range(1, PLANE):
        w_q(d).start()
    for k in range(1, chunks):
        second_of(k)

    for d in range(1, PLANE):
        w_q(d).wait_recv()
    loads[3].wait()

    def gate_tile(t, carry):
        a, j = t // row_tiles, t % row_tiles
        rows = pl.ds(j * tile, tile)
        weight = wf[...].reshape(width, width)
        g = jnp.dot(tok[a, rows, :], weight, preferred_element_type=F32).astype(BF16)
        gate[a, rows, :] = g
        gf = g.astype(F32)
        up = cot[a, rows, :].astype(F32) * (gf * jax.nn.sigmoid(gf))
        sends = per // chunks
        sg_s[a, pl.ds(j * sends, sends)] = up.astype(BF16).reshape(sends, chunks, ROWS, width)
        return carry

    lax.fori_loop(0, blocks * row_tiles, gate_tile, 0)
    send_second_grad(0)

    for k in range(chunks):
        each(functools.partial(to_rows_, 2, k, sc, sr), "recv")

    def delta_tile(t, carry):
        a, j = t // row_tiles, t % row_tiles
        rows = pl.ds(j * tile, tile)
        gf = gate[a, rows, :].astype(F32)
        sig = jax.nn.sigmoid(gf)
        sec = sr[a, pl.ds(j * per, per)].reshape(tile, width).astype(F32)
        up = cot[a, rows, :].astype(F32)
        out[a, rows, :] = (sec * (gf * sig)).astype(BF16)
        delta[a, rows, :] = (up * sec * (sig * (1.0 + gf * (1.0 - sig)))).astype(BF16)
        return carry

    lax.fori_loop(0, blocks * row_tiles, delta_tile, 0)
    out_copy = pltpu.make_async_copy(out, out_hbm, lsem.at[0])
    out_copy.start()

    def weight_tile(z, carry):
        cols = pl.ds(pl.multiple_of(z * tile, tile), tile)
        tokens_2d = tok[:, :, cols].reshape(blocks * tok.shape[1], tile)
        delta_2d = delta[...].reshape(blocks * tok.shape[1], width)
        prod = lax.dot_general(tokens_2d, delta_2d, (((0,), (0,)), ((), ())), preferred_element_type=F32)
        wt[z] = prod.astype(BF16).reshape(PLANE, tile // PLANE, width)
        return carry

    lax.fori_loop(0, width // tile, weight_tile, 0)

    def g_q(d):
        peer = (qi + d) % PLANE
        return remote(wt.at[:, peer], half.at[d - 1], gs_sem.at[0, d], gr_sem.at[0, d], zi * PLANE + peer)

    g_near = [
        remote(quarter.at[beside], tail.at[0], gs_sem.at[1, 0], gr_sem.at[1, 0], beside * PLANE + qi),
        remote(
            quarter.at[(beside + nz // 2) % nz], tail.at[1], gs_sem.at[1, 1], gr_sem.at[1, 1], beside * PLANE + qi
        ),
    ]
    g_far = remote(pair, tail.at[2], gs_sem.at[1, 2], gr_sem.at[1, 2], across * PLANE + qi)

    for d in range(1, PLANE):
        g_q(d).start()

    for k in range(1, chunks):
        send_second_grad(k)

    for d in range(1, PLANE):
        g_q(d).wait_recv()

    def sum_tile(z, carry):
        total = wt[z, qi].astype(F32)
        for d in range(PLANE - 1):
            total = total + half[d, z].astype(F32)
        quarter[z] = total.astype(BF16)
        return carry

    lax.fori_loop(0, nz, sum_tile, 0)
    for copy in g_near:
        copy.start()
    first_grad_of(0)

    for copy in g_near:
        copy.wait_recv()
    pair[...] = (quarter[across].astype(F32) + tail[1].astype(F32)).astype(BF16)
    g_far.start()
    for k in range(1, chunks):
        first_grad_of(k)

    def part_tile(t, carry):
        a, j = t // row_tiles, t % row_tiles
        rows = pl.ds(j * tile, tile)
        weight = wf[...].reshape(width, width)
        part[a, rows, :] = lax.dot_general(
            delta[a, rows, :], weight, (((1,), (1,)), ((), ())), preferred_element_type=F32
        ).astype(BF16)
        return carry

    lax.fori_loop(0, blocks * row_tiles, part_tile, 0)
    part_copy = pltpu.make_async_copy(part, part_hbm, lsem.at[1])
    part_copy.start()

    scale_w = width ** (-0.5)
    for k in range(chunks):
        pairs = lax.dot_general(
            gc[k].reshape(deep, width), fc[k].reshape(deep, width),
            (((1,), (1,)), ((), ())), preferred_element_type=F32,
        )
        kept = jnp.where(same, pairs * scale_w, 0.0).astype(BF16)
        picked = lax.dot_general(
            kept, spread, (((1,), (1,)), ((), ())), preferred_element_type=F32
        ).astype(BF16)
        rgrad[k] = lax.dot_general(
            turn, picked, (((0,), (0,)), ((), ())), preferred_element_type=F32
        ).astype(BF16)

    g_far.wait_recv()
    total = quarter[zi].astype(F32) + tail[0].astype(F32) + tail[2].astype(F32)
    ggrad[...] = total * (blocks * tok.shape[1] * n) ** (-0.5)

    for k in range(chunks):
        each(functools.partial(to_rows_, 3, k, fgc, fr), "recv")
        pltpu.make_async_copy(
            fgc.at[k, pl.ds(me * blocks, blocks)], fr.at[:, me * chunks + k], lsem.at[4 + k]
        ).wait()
    out_copy.wait()
    part_copy.wait()

    for k in range(chunks):
        each(functools.partial(to_cols, 0, k, first_s, fc), "send")
        each(functools.partial(to_cols, 1, k, sg_s, gc), "send")
        each(functools.partial(to_rows_, 2, k, sc, sr), "send")
        each(functools.partial(to_rows_, 3, k, fgc, fr), "send")
    for copy in (w_far, w_near, w_pass, *g_near, g_far):
        copy.wait_send()
    for d in range(1, PLANE):
        w_q(d).wait_send()
        g_q(d).wait_send()


def last_kernel(scale_w, tok, left, fr, part, out_in, ggrad_in, rgrad_in, out, igrad, lgrad, ggrad, rgrad):
    size = part.shape[1]
    rows = pl.ds(pl.multiple_of((pl.program_id(0) % (tok.shape[1] // size)) * size, size), size)
    out[...] = out_in[...]
    ggrad[...] = ggrad_in[...]
    rgrad[...] = rgrad_in[...]
    lg = lax.dot_general(fr[0, rows, :], tok[0], (((1,), (1,)), ((), ())), preferred_element_type=F32)
    lgrad[0] = (lg * scale_w).astype(BF16)
    mixer = lax.dot_general(left[0], fr[0], (((0,), (0,)), ((), ())), preferred_element_type=F32)
    igrad[0] = (mixer + part[0].astype(F32)).astype(BF16)


def fused_body(n, tokens, cotangent, gate_weight, left_blocks, right_blocks):
    blocks, inner = left_blocks.shape[0], left_blocks.shape[1]
    own, outer = right_blocks.shape[0], right_blocks.shape[1]
    width = tokens.shape[1]
    chunks = own // ROWS
    groups = inner // ROWS
    deep = outer * ROWS
    nz = n // PLANE
    shard = width // n
    rows = (blocks, inner, width)
    by_row = pltpu.VMEM((blocks, groups, ROWS, width), BF16)
    by_peer = pltpu.VMEM((blocks, n, chunks, ROWS, width), BF16)
    by_col = pltpu.VMEM((chunks, outer, ROWS, width), BF16)
    vmem = pl.BlockSpec(memory_space=pltpu.VMEM)
    hbm = pl.BlockSpec(memory_space=pltpu.HBM)
    token_grid = tokens.reshape(rows)
    out, part, fr, ggrad, rgrad = pl.pallas_call(
        functools.partial(mixer_kernel, n),
        out_shape=(
            jax.ShapeDtypeStruct(rows, BF16),
            jax.ShapeDtypeStruct(rows, BF16),
            jax.ShapeDtypeStruct((blocks, groups, ROWS, width), BF16),
            jax.ShapeDtypeStruct((shard, width), F32),
            jax.ShapeDtypeStruct((chunks, deep, outer), BF16),
        ),
        in_specs=[hbm, hbm, hbm, hbm, vmem],
        out_specs=[hbm, hbm, hbm, vmem, vmem],
        scratch_shapes=[
            pltpu.VMEM(rows, BF16),
            pltpu.VMEM(rows, BF16),
            pltpu.VMEM((blocks, n, chunks, ROWS, inner), BF16),
            pltpu.VMEM(rows, BF16),
            pltpu.VMEM(rows, BF16),
            pltpu.VMEM((nz, PLANE, shard, width), BF16),
            by_peer, by_peer, by_col, by_col, by_col, by_col, by_row,
            pltpu.VMEM(rows, BF16),
            pltpu.VMEM(rows, BF16),
            pltpu.VMEM((nz, PLANE, shard, width), BF16),
            pltpu.VMEM((PLANE - 1, nz, shard, width), BF16),
            pltpu.VMEM((nz, shard, width), BF16),
            pltpu.VMEM((shard, width), BF16),
            pltpu.VMEM((3, shard, width), BF16),
            pltpu.VMEM((chunks, deep, deep), BF16),
            pltpu.SemaphoreType.DMA((4, chunks, n)),
            pltpu.SemaphoreType.DMA((4, chunks, n)),
            pltpu.SemaphoreType.DMA((2, PLANE)),
            pltpu.SemaphoreType.DMA((2, PLANE)),
            pltpu.SemaphoreType.DMA((2, PLANE)),
            pltpu.SemaphoreType.DMA((2, PLANE)),
            pltpu.SemaphoreType.DMA((4 + chunks,)),
        ],
        compiler_params=pltpu.CompilerParams(
            collective_id=0, has_side_effects=True, vmem_limit_bytes=60 * 2**20
        ),
    )(
        token_grid, cotangent.reshape(rows), gate_weight,
        left_blocks.reshape(blocks, n, chunks, ROWS, inner), right_blocks.reshape(chunks, deep, outer),
    )
    size = 256
    per_block = inner // size
    steps = blocks * per_block
    tall = pl.BlockSpec((1, inner, width), lambda t: (t // per_block, 0, 0))
    flat = pl.BlockSpec((1, size, width), lambda t: (t // per_block, t % per_block, 0))
    square = pl.BlockSpec((1, size, inner), lambda t: (t // per_block, t % per_block, 0))
    side = pl.BlockSpec((1, inner, size), lambda t: (t // per_block, 0, t % per_block))
    weight_spec = pl.BlockSpec((shard // steps, width), lambda t: (t, 0))
    right_spec = pl.BlockSpec((own * outer // steps, outer), lambda t: (t, 0))
    out, igrad, lgrad, ggrad, rgrad = pl.pallas_call(
        functools.partial(last_kernel, width ** (-0.5)),
        grid=(steps,),
        out_shape=(
            jax.ShapeDtypeStruct(rows, BF16),
            jax.ShapeDtypeStruct(rows, BF16),
            jax.ShapeDtypeStruct((blocks, inner, inner), BF16),
            jax.ShapeDtypeStruct((shard, width), F32),
            jax.ShapeDtypeStruct((own * outer, outer), BF16),
        ),
        in_specs=[tall, side, tall, flat, flat, weight_spec, right_spec],
        out_specs=[flat, flat, square, weight_spec, right_spec],
    )(token_grid, left_blocks, fr.reshape(rows), part, out, ggrad, rgrad.reshape(own * outer, outer))
    rgrad = rgrad.reshape(own, outer, outer)
    return (out.reshape(tokens.shape), igrad.reshape(tokens.shape), ggrad, lgrad, rgrad)


def chosen_body(tokens, cotangent, gate_weight, left_blocks, right_blocks):
    n = lax.axis_size("seq")
    own, width, inner = right_blocks.shape[0], tokens.shape[1], left_blocks.shape[1]
    if n == PLANE * PLANE and own % ROWS == 0 and width == 256 * PLANE and inner % 256 == 0:
        return fused_body(n, tokens, cotangent, gate_weight, left_blocks, right_blocks)
    return body(tokens, cotangent, gate_weight, left_blocks, right_blocks)


def solution(mesh):
    in_specs = (
        P(("groups", "seq"), None),
        P(("groups", "seq"), None),
        P("seq", None),
        P("seq", None, None),
        P("seq", None, None),
    )
    out_specs = (
        P(("groups", "seq"), None),
        P(("groups", "seq"), None),
        P(("groups", "seq"), None),
        P(("groups", "seq"), None, None),
        P(("groups", "seq"), None, None),
    )
    return jax.shard_map(chosen_body, mesh=mesh, in_specs=in_specs, out_specs=out_specs, check_vma=False)
```
